256 devices in a mesh: pulse: 8 (over y, core), tile: 32 (over x, z).
Axes of the slice: x: 4, y: 4, z: 8, core: 2. Of those that a mesh axis runs over, the one named last changes fastest.
Arguments:
- echoes: bfloat16 [512, 2, 2, 16384], P(('pulse', 'tile')), may hold values from -6 to 6
- pulse_slope: bfloat16 [512, 2], P(('pulse', 'tile')), may hold values from -0.023925781 to 0.023925781
- pulse_shift: bfloat16 [512, 2], P(('pulse', 'tile')), may hold values from -3.140625 to 3.140625
- footprint: int32 [8, 32, 32], P('pulse'), may hold values from -1 to 63, as said below
- band_start: int32 [1024], P('tile'), may hold values from 0 to 13216
- row_phase: float32 [1024], P('tile'), may hold values from -1 to 1
Outputs:
- formed_image: float32 [2, 1024, 4096], P(None, 'tile', 'pulse')
The draws below stay inside these ranges and needn't reach their ends.
Inputs may be any that keep to these rules, and one draw needn't show every extreme that they name: footprint[g, t] lists in rising order the numbers of group g's blocks whose echoes reach row strip t, then -1 to the end. It names at most one block of each run of 2 numbers that starts at a multiple of 2. In every group some list has 32 entries.
All inputs are finite; a program needn't handle non-finite values.
Results may differ from the reference program's by a relative error of at most 0.0039.
Values may be sent and summed in bfloat16 or wider, within the bound.
No kernel may reach another device: no remote copies, remote signals or barrier semaphores. Data moves between devices by JAX's collectives and lax.ppermute only.
A program may use at most 64 MiB of HBM per device.

```python
import jax
import jax.numpy as jnp
from jax import lax

R = 16384
NCOL = 4096
TR = 32
PB = 2
BLK_DEV = 2
ITERS = 2
GROUPS = 8
STRIPS = 32
WINDOW = 3168
GROUP_BLOCKS = 64
NBLOCKS = 512
NROW = 1024
LIST = 32


def draw_footprint(key, part):
    pick_key = jax.random.fold_in(key, 11)
    heavy_key = jax.random.fold_in(key, 12)
    member_key = jax.random.fold_in(key, 13)
    picked = jax.random.randint(pick_key, (GROUPS, STRIPS, STRIPS), 0, 10) < 4
    heavy_strip = jax.random.randint(heavy_key, (GROUPS,), 0, STRIPS)
    strip_ids = jnp.arange(STRIPS, dtype=jnp.int32)
    is_heavy = strip_ids[None, :, None] == heavy_strip[:, None, None]
    picked = picked | is_heavy
    member = jax.random.randint(member_key, (GROUPS, STRIPS, STRIPS), 0, BLK_DEV)
    last_source = strip_ids[None, None, :] == STRIPS - 1
    member = jnp.where(is_heavy & last_source, BLK_DEV - 1, member)
    block_ids = strip_ids[None, None, :] * BLK_DEV + member
    sort_keys = jnp.where(picked, block_ids, BLK_DEV * STRIPS + block_ids)
    ordering = jnp.argsort(sort_keys, axis=-1)
    sorted_ids = jnp.take_along_axis(block_ids, ordering, axis=-1)
    sorted_used = jnp.take_along_axis(picked, ordering, axis=-1)
    return jnp.where(sorted_used, sorted_ids, -1).astype(jnp.int32)


def touch_ends(result, key, low, largest):
    extent = result.shape
    place = [jax.random.randint(jax.random.fold_in(key, axis), (), 0, extent[axis]) for axis in range(len(extent))]
    result = result.at[tuple(place)].set(low)
    longest = extent.index(max(extent))
    place[longest] = (place[longest] + 1) % extent[longest]
    return result.at[tuple(place)].set(largest)


def levels(rng, shape, pieces, low, top_value):
    factor_of = 1.0
    for axis_at, parts in pieces:
        heights = jax.random.uniform(jax.random.fold_in(jax.random.fold_in(rng, 6), axis_at), (parts,), jnp.float32, low / len(pieces), top_value / len(pieces))
        factor_of = factor_of * jnp.repeat(jnp.exp(heights), shape[axis_at] // parts).reshape((-1,) + (1,) * (len(shape) - 1 - axis_at))
    return factor_of


def bell_draw(own_key, shape, deviation, reach, split=(), kind=jnp.bfloat16):
    result = deviation * jax.random.normal(own_key, shape, jnp.float32)
    if split:
        result = result * levels(own_key, shape, split, -0.22, 0.18)
    return jnp.clip(result, -reach, reach).astype(kind)


def setup_inputs(seed: int = 0) -> dict:
    streams_of = jax.random.split(jax.random.key(seed), 7)
    return {
        "echoes": bell_draw(streams_of[0], (NBLOCKS, PB, 2, R), 1.0, 6.0, ((0, 256),)),
        "pulse_slope": jnp.clip(jax.random.uniform(streams_of[1], (NBLOCKS, PB), jnp.float32, -0.023925781, 0.023925781) * levels(streams_of[1], (NBLOCKS, PB), ((0, 256),), -0.4, 0.0), -0.023925781, 0.023925781).astype(jnp.bfloat16),
        "pulse_shift": jnp.clip(jax.random.uniform(streams_of[2], (NBLOCKS, PB), jnp.float32, -3.140625, 3.140625), -3.140625, 3.140625).astype(jnp.bfloat16),
        "footprint": draw_footprint(jax.random.fold_in(streams_of[6], 71), 0),
        "band_start": touch_ends(jax.random.randint(streams_of[4], (NROW,), 0, R - WINDOW + 1), jax.random.fold_in(streams_of[4], 1), 0, R - WINDOW).astype(jnp.int32),
        "row_phase": jnp.clip(jax.random.uniform(streams_of[5], (NROW,), jnp.float32, -1.0, 1.0) * levels(streams_of[5], (NROW,), ((0, 32),), -0.4, 0.0), -1.0, 1.0),
    }


step_size = 0.5
tv_weight = 0.4
floor_square = 0.25

def cubic_table():
    columns = jnp.arange(128, dtype=jnp.int32)
    quarter_pos = 3 * columns + 4
    base_tap = quarter_pos // 4
    fraction = (quarter_pos % 4).astype(jnp.float32) / 4.0
    fraction_sq = fraction * fraction
    fraction_cube = fraction_sq * fraction
    weights = [(-fraction_cube + 2.0 * fraction_sq - fraction) * 0.5, (3.0 * fraction_cube - 5.0 * fraction_sq + 2.0) * 0.5, (-3.0 * fraction_cube + 4.0 * fraction_sq + fraction) * 0.5, (fraction_cube - fraction_sq) * 0.5]
    tap_rows = jnp.arange(128, dtype=jnp.int32)[:, None]
    cubic_weights = jnp.zeros((128, 128), jnp.float32)
    for tap_shift, weight in zip(range(-1, 3), weights):
        cubic_weights = cubic_weights + jnp.where(tap_rows == (base_tap + tap_shift)[None, :], weight[None, :], 0.0)
    return cubic_weights

def block_image(block_echo, block_slope, block_shift, band_start, row_phase, cubic_weights):
    pulses = block_echo.shape[0]
    row_count = band_start.shape[0]
    col_blocks = NCOL // 128
    window_span = 96 * (col_blocks + 1)
    flat_echo = block_echo.reshape(pulses * 2, block_echo.shape[2])
    segments = jax.vmap(lambda row_start: lax.dynamic_slice_in_dim(flat_echo, row_start, window_span, axis=1))(band_start)
    leading = segments[..., :96 * col_blocks].reshape(row_count, pulses * 2, col_blocks, 96)
    trailing = segments[..., 96:].reshape(row_count, pulses * 2, col_blocks, 96)[..., :32]
    windows = jnp.concatenate([leading, trailing], axis=-1)
    windows = jnp.transpose(windows, (0, 2, 1, 3)).reshape(row_count, col_blocks, pulses, 2, 128).astype(jnp.float32)
    slopes = block_slope.astype(jnp.float32)
    shifts = block_shift.astype(jnp.float32)
    block_pos = (128 * jnp.arange(col_blocks, dtype=jnp.int32)).astype(jnp.float32)
    angle_grid = shifts[None, None, :] * row_phase[:, None, None] + slopes[None, None, :] * block_pos[None, :, None]
    cosine = jnp.cos(angle_grid)[..., None]
    sines = jnp.sin(angle_grid)[..., None]
    real_part = windows[:, :, :, 0]
    imag_part = windows[:, :, :, 1]
    turned_re = real_part * cosine - imag_part * sines
    turned_im = real_part * sines + imag_part * cosine
    turned = jnp.stack([turned_re, turned_im], axis=3).astype(jnp.bfloat16).reshape(row_count * col_blocks, pulses * 256)
    column_pos = jnp.arange(128, dtype=jnp.int32).astype(jnp.float32)
    column_ramp = slopes[:, None] * column_pos[None, :]
    kernel_re = cubic_weights[None] * jnp.cos(column_ramp)[:, None, :]
    kernel_im = cubic_weights[None] * jnp.sin(column_ramp)[:, None, :]
    upper_rows = jnp.concatenate([kernel_re, kernel_im], axis=2)
    bottom = jnp.concatenate([-kernel_im, kernel_re], axis=2)
    kernel = jnp.stack([upper_rows, bottom], axis=1).astype(jnp.bfloat16).reshape(pulses * 256, 256)
    product = jnp.dot(turned, kernel, preferred_element_type=jnp.float32)
    return product.reshape(row_count, col_blocks, 256)

def tv_update(field, padded, base_image, row_anchor, col_anchor, grid_rows, grid_cols):
    row_count = field.shape[1]
    col_count = field.shape[2]
    grad_rows = padded[:, 1:row_count + 2, 0:col_count + 1] - padded[:, 0:row_count + 1, 0:col_count + 1]
    grad_cols = padded[:, 0:row_count + 1, 1:col_count + 2] - padded[:, 0:row_count + 1, 0:col_count + 1]
    row_ids = row_anchor - 1 + jnp.arange(row_count + 1, dtype=jnp.int32)
    col_ids = col_anchor - 1 + jnp.arange(col_count + 1, dtype=jnp.int32)
    inside = (row_ids >= 0)[:, None] & (col_ids >= 0)[None, :]
    grad_rows = jnp.where((inside & (row_ids < grid_rows - 1)[:, None])[None], grad_rows, 0.0)
    grad_cols = jnp.where((inside & (col_ids < grid_cols - 1)[None, :])[None], grad_cols, 0.0)
    magnitude = jnp.sqrt(lax.optimization_barrier(jnp.sum(grad_rows * grad_rows + grad_cols * grad_cols, axis=0)) + floor_square)
    flux_rows = grad_rows / magnitude[None]
    flux_cols = grad_cols / magnitude[None]
    divergence = flux_rows[:, 1:, 1:] - flux_rows[:, :-1, 1:] + flux_cols[:, 1:, 1:] - flux_cols[:, 1:, :-1]
    return field - step_size * (field - base_image - tv_weight * divergence)

def reference(echoes, pulse_slope, pulse_shift, footprint, band_start, row_phase):
    cubic_weights = cubic_table()
    col_blocks = NCOL // 128

    def strip_image(strip_index):
        starts = lax.dynamic_slice_in_dim(band_start, strip_index * TR, TR)
        phases = lax.dynamic_slice_in_dim(row_phase, strip_index * TR, TR)
        entries = lax.dynamic_index_in_dim(footprint, strip_index, axis=1, keepdims=False).reshape(-1)
        group_ids = jnp.repeat(jnp.arange(GROUPS, dtype=jnp.int32), LIST)

        def add_block(running, list_entry):
            group_index, block_id = list_entry

            def used_branch(partial_sum):
                global_id = (group_index * GROUP_BLOCKS + block_id).astype(jnp.int32)
                block_echo = lax.dynamic_index_in_dim(echoes, global_id, 0, keepdims=False)
                block_slope = lax.dynamic_index_in_dim(pulse_slope, global_id, 0, keepdims=False)
                block_shift = lax.dynamic_index_in_dim(pulse_shift, global_id, 0, keepdims=False)
                return partial_sum + block_image(block_echo, block_slope, block_shift, starts, phases, cubic_weights)
            return (lax.cond(block_id >= 0, used_branch, lambda partial_sum: partial_sum, running), None)
        zero_image = jnp.zeros((TR, col_blocks, 256), jnp.float32)
        running, _ = lax.scan(add_block, zero_image, (group_ids, entries))
        return running
    strips_out = lax.map(strip_image, jnp.arange(STRIPS, dtype=jnp.int32))
    real_plane = strips_out[..., :128].reshape(NROW, NCOL)
    imag_plane = strips_out[..., 128:].reshape(NROW, NCOL)
    normalize = (PB * STRIPS * GROUPS) ** (-0.5)
    base_image = jnp.stack([real_plane, imag_plane]) * normalize
    field = base_image
    for iteration in range(ITERS):
        padded = jnp.pad(field, ((0, 0), (1, 1), (1, 1)))
        field = tv_update(field, padded, base_image, 0, 0, NROW, NCOL)
    return field
```

```python
import functools

import jax
import jax.numpy as jnp
from jax import lax
from jax.experimental import pallas as pl
from jax.experimental.pallas import tpu as pltpu
from jax.sharding import Mesh, PartitionSpec as P

NCOL = 4096
PB = 2
ITERS = 2
TR = 32
STEP = 0.5
TV_WEIGHT = 0.4
FLOOR_SQ = 0.25
F32 = jnp.float32
BF16 = jnp.bfloat16
PITCH = 33
PIECE = 304
UNROLL = (8, 8, 8, 8, 4, 4, 4, 4)


def cubic_pair():
    j = lax.broadcasted_iota(jnp.int32, (256, 256), 0)
    c = lax.broadcasted_iota(jnp.int32, (256, 256), 1)
    same = (j < 128) == (c < 128)
    q = 3 * (c & 127) + 4
    f = (q & 3).astype(F32) / 4.0
    f2 = f * f
    f3 = f2 * f
    weights = [
        (-f3 + 2.0 * f2 - f) * 0.5,
        (3.0 * f3 - 5.0 * f2 + 2.0) * 0.5,
        (-3.0 * f3 + 4.0 * f2 + f) * 0.5,
        (f3 - f2) * 0.5,
    ]
    tap = (j & 127) - q // 4
    out = jnp.zeros((256, 256), F32)
    for shift, weight in zip(range(-1, 3), weights):
        out = out + jnp.where(same & (tap == shift), weight, 0.0)
    return out.astype(BF16)


def form_kernel(
    n_in, strips, slots, sets, bs_ref, cnt_ref, lst_ref, core_ref, are_ref, aim_ref, *refs
):
    e_refs = refs[:n_in]
    w_ref, tre_ref, tim_ref, own_ref, oth_ref, e_s, o_s = refs[n_in:]
    row = 0
    for e in e_refs:
        e_s[row : row + 512, :] = e[0:512, :].astype(F32)
        row += 512
    maxn = lst_ref.shape[0] // sets
    half_o = strips * 40 * PITCH
    lane = lax.broadcasted_iota(jnp.int32, (8, 128), 1)
    lane16 = lax.broadcasted_iota(jnp.int32, (16, 128), 1)

    def zero_rows(first, count):
        def step(k, carry):
            at = (first + k) * PITCH
            o_s[pl.ds(at, 32), :] = jnp.zeros((32, 128), F32)
            o_s[pl.ds(at + half_o, 32), :] = jnp.zeros((32, 128), F32)
            return carry

        lax.fori_loop(0, count, step, 0)

    for s in range(strips):
        zero_rows(s * 40 + 34, 4)

    def one_set(t, carry):
        cnt = cnt_ref[t]
        is_main = t < strips
        edge = t - strips
        strip = jnp.where(is_main, t, edge & (strips - 1))
        below = edge >= strips
        nrow = jnp.where(is_main, TR, 2)
        orow = strip * 40 + jnp.where(is_main, 0, jnp.where(below, 32, 38))
        part = jnp.where(is_main, 0, jnp.where(below, 2, 1))
        brow = strip * TR + jnp.where(part == 1, TR - 2, 0)
        acol = part * 128 + brow

        @pl.when(cnt == 0)
        def _():
            zero_rows(orow, nrow)

        for n, unroll, here in [(n, UNROLL[n - 1], is_main) for n in range(1, maxn + 1)] + [
            (n, 2, edge >= 0) for n in range(1, maxn + 1) if UNROLL[n - 1] != 2
        ]:
            if unroll != 2 or UNROLL[n - 1] != 2:
                here = here & (cnt == n)
            else:
                here = cnt == n

            @pl.when(here)
            def _(n=n, unroll=unroll):
                slot = [lst_ref[t * maxn + j] for j in range(n)]

                def some_rows(step, carry):
                    left, right = [], []
                    for u in range(unroll):
                        bs = bs_ref[part, brow + step * unroll + u]
                        for i in range(4):
                            start = bs + 96 * i
                            m = lax.shift_right_logical(start, 7)
                            o = start & 127
                            back = (128 - o) & 127
                            whole = lane16 < 128 - o
                            for j in range(n):
                                for ri, side in ((0, left), (1, right)):
                                    at = slot[j] * 512 + ri * 128 + m
                                    lo, hi = [
                                        jnp.concatenate(
                                            [
                                                e_s[pl.ds(at + t, 8, stride=3), :],
                                                e_s[pl.ds(at + t + 256, 8, stride=3), :],
                                            ],
                                            axis=0,
                                        ).astype(BF16)
                                        for t in range(2)
                                    ]
                                    lo = pltpu.roll(lo, back, 1)
                                    hi = pltpu.roll(hi, back, 1)
                                    side.append(jnp.where(whole, lo, hi))
                    lhs = jnp.concatenate(
                        [jnp.concatenate(left, axis=0), jnp.concatenate(right, axis=0)], axis=1
                    )
                    res = jnp.dot(lhs, w_ref[...], preferred_element_type=F32)
                    for u in range(unroll):
                        r = step * unroll + u
                        acc_re = [None] * 4
                        acc_im = [None] * 4
                        for j in range(n):
                            for p in range(2):
                                pa = slot[j] * 2 + p
                                a_re = are_ref[pa, acol + r]
                                a_im = aim_ref[pa, acol + r]
                                for i in range(4):
                                    t_re = tre_ref[pa, i]
                                    t_im = tim_ref[pa, i]
                                    b_re = a_re * t_re - a_im * t_im
                                    b_im = a_re * t_im + a_im * t_re
                                    row0 = (((u * 4 + i) * n + j) * 2 + p) * 8
                                    x_re = res[row0 : row0 + 8, :128]
                                    x_im = res[row0 : row0 + 8, 128:]
                                    y_re = b_re * x_re - b_im * x_im
                                    y_im = b_re * x_im + b_im * x_re
                                    first = j == 0 and p == 0
                                    acc_re[i] = y_re if first else acc_re[i] + y_re
                                    acc_im[i] = y_im if first else acc_im[i] + y_im
                        for i in range(4):
                            at = (orow + r) * PITCH + i * 8
                            o_s[pl.ds(at, 8), :] = acc_re[i]
                            o_s[pl.ds(at + half_o, 8), :] = acc_im[i]
                    return carry

                lax.fori_loop(0, lax.shift_right_logical(nrow, unroll.bit_length() - 1), some_rows, 0)

        return carry

    lax.fori_loop(0, sets, one_set, 0)

    core = core_ref[0]
    sub = lax.broadcasted_iota(jnp.int32, (8, 128), 0)
    edge_rows = (sub < 2) | (sub >= 6)

    def pack(s, y, c):
        q = 2 * y + c
        base = s * (40 * PITCH) + q
        base_after = s * (40 * PITCH) + jnp.minimum(q + 1, 7)
        base_before = s * (40 * PITCH) + jnp.maximum(q - 1, 0)

        def fetch(plane, at, rg, i):
            return o_s[pl.ds(at + (plane * half_o + rg * 8 * PITCH + i * 8), 8, stride=PITCH), :]

        out = []
        for plane in range(2):
            for rg in range(4):
                for i in range(4):
                    out.append(fetch(plane, base, rg, i))
        for i in range(4):
            out.append(
                jnp.where(edge_rows, fetch(0, base, 4, i), pltpu.roll(fetch(1, base, 4, i), 4, 0))
            )
        cols = jnp.zeros((8, 128), F32)
        for plane in range(2):
            for rg in range(5):
                after = fetch(plane, base_after, rg, 0)
                before = fetch(plane, base_before, rg, 3)
                k = plane * 5 + rg
                both = pltpu.roll(jnp.where(lane < 64, after, before), 2 + 4 * k, 1)
                cols = jnp.where(lax.shift_right_logical(lane, 2) == k, both, cols)
        out.append(cols)
        out.append(jnp.zeros((8, 128), F32))
        return jnp.concatenate(out, axis=0)

    def pack_dest(d, carry):
        s = lax.shift_right_logical(d, 2)
        y = d & 3
        own_ref[d] = pack(s, y, core)
        oth_ref[d] = pack(s, y, 1 - core).astype(BF16)
        return carry

    lax.fori_loop(0, strips * 4, pack_dest, 0)


def form_images(e_list, w, t_re, t_im, bs, cnt, lst, core, a_re, a_im, strips):
    sets = cnt.shape[0]
    slots = t_re.shape[0] // 2
    smem = pl.BlockSpec(memory_space=pltpu.SMEM)
    vmem = pl.BlockSpec(memory_space=pltpu.VMEM)
    n_in = len(e_list)
    dests = strips * 4
    return pl.pallas_call(
        functools.partial(form_kernel, n_in, strips, slots, sets),
        out_shape=(
            jax.ShapeDtypeStruct((dests, PIECE, 128), F32),
            jax.ShapeDtypeStruct((dests, PIECE, 128), BF16),
        ),
        in_specs=[smem] * 6 + [vmem] * (n_in + 3),
        out_specs=(vmem, vmem),
        scratch_shapes=[
            pltpu.VMEM((slots * 512, 128), F32),
            pltpu.VMEM((2 * strips * 40 * PITCH + 8, 128), F32),
        ],
        compiler_params=pltpu.CompilerParams(vmem_limit_bytes=48 * 1024 * 1024),
        name="form_images",
    )(bs, cnt, lst, core, a_re, a_im, *e_list, w, t_re, t_im)


def tables_kernel(nz, at_ref, gs_ref, g_ref, tre_ref, tim_ref, are_ref, aim_ref, bs_ref):
    x, z = at_ref[0], at_ref[1]
    sub = lax.broadcasted_iota(jnp.int32, (8, 128), 0)
    lane = lax.broadcasted_iota(jnp.int32, (8, 128), 1)
    prev = lax.rem(z + nz - 1, nz)
    nxt = lax.rem(z + 1, nz)

    def lines(which):
        own = g_ref[pl.ds(3 * z + which, 1), :]
        above = g_ref[pl.ds(3 * prev + which, 1), :]
        below = g_ref[pl.ds(3 * nxt + which, 1), :]
        above = jnp.where(z == 0, pltpu.roll(above, 32, 1), above)
        below = jnp.where(z == nz - 1, pltpu.roll(below, 96, 1), below)
        return [jnp.broadcast_to(v, (8, 128)) for v in (own, above, below)]

    first = lines(0)
    bs_ref[...] = jnp.where(sub == 0, first[0], jnp.where(sub == 1, first[1], first[2])).astype(jnp.int32)
    phase = lines(1)
    place = (512 * sub + lane).astype(F32)
    for d in range(nz):
        src = 3 * lax.rem(z + nz - d, nz) + 2
        for mem in range(2):
            for p in range(2):
                k = (d * 2 + mem) * 2 + p
                slope = gs_ref[src, 32 * x + mem * 4 + p]
                ang = slope * place
                t_re, t_im = jnp.cos(ang), jnp.sin(ang)
                turn = jnp.full((8, 128), slope * 128.0, F32)
                e_re, e_im = jnp.cos(turn), jnp.sin(turn)
                for i in range(4):
                    tre_ref[k, i] = t_re
                    tim_ref[k, i] = t_im
                    if i < 3:
                        t_re, t_im = t_re * e_re - t_im * e_im, t_re * e_im + t_im * e_re
    for grp in range(nz // 2):
        shift = jnp.zeros((8, 128), F32)
        for row in range(8):
            k = grp * 8 + row
            d, mem, p = k // 4, (k // 2) % 2, k % 2
            src = 3 * lax.rem(z + nz - d, nz) + 2
            shift = jnp.where(sub == row, gs_ref[src, 32 * x + mem * 4 + 2 + p], shift)
        for part in range(3):
            ang = shift * phase[part]
            are_ref[grp * 8 : grp * 8 + 8, part * 128 : part * 128 + 128] = jnp.cos(ang)
            aim_ref[grp * 8 : grp * 8 + 8, part * 128 : part * 128 + 128] = jnp.sin(ang)


def tables(at, g, nz):
    smem = pl.BlockSpec(memory_space=pltpu.SMEM)
    vmem = pl.BlockSpec(memory_space=pltpu.VMEM)
    pulses = 4 * nz
    wave = jax.ShapeDtypeStruct((pulses, 4, 8, 128), F32)
    turn = jax.ShapeDtypeStruct((pulses, 384), F32)
    return pl.pallas_call(
        functools.partial(tables_kernel, nz),
        out_shape=(wave, wave, turn, turn, jax.ShapeDtypeStruct((8, 128), jnp.int32)),
        in_specs=[smem, smem, vmem],
        out_specs=(vmem,) * 5,
        name="tables",
    )(at, g, g)


def refine_kernel(norm, nrow, ncol, pos_ref, got_ref, out_ref):
    total = got_ref[0].astype(F32)
    for d in range(1, got_ref.shape[0]):
        total = total + got_ref[d].astype(F32)
    total = total * norm
    cols = total[288:296]
    planes = []
    for plane in range(2):
        rows = []
        for rg in range(5):
            if rg < 4:
                at = [((plane * 4 + rg) * 4 + i) * 8 for i in range(4)]
                line = [total[k : k + 8] for k in at]
            else:
                line = [total[256 + i * 8 : 264 + i * 8] for i in range(4)]
                if plane == 1:
                    line = [pltpu.roll(v, 4, 0) for v in line]
            k = plane * 5 + rg
            line.append(pltpu.roll(cols, (126 - 4 * k) % 128, 1))
            rows.append(jnp.concatenate(line, axis=1))
        planes.append(jnp.concatenate(rows, axis=0))
    h, w = 40, 640
    j = lax.broadcasted_iota(jnp.int32, (h, w), 0)
    c = lax.broadcasted_iota(jnp.int32, (h, w), 1)
    rid = pos_ref[0] + jnp.where(j >= 36, j - 40, j)
    cid = pos_ref[1] + jnp.where(c >= 576, c - 640, c)
    inside = (rid >= 0) & (cid >= 0) & (rid < nrow) & (cid < ncol)
    ok_r = inside & (rid < nrow - 1)
    ok_c = inside & (cid < ncol - 1)
    field = list(planes)
    for _ in range(ITERS):
        gr = [jnp.where(ok_r, pltpu.roll(f, h - 1, 0) - f, 0.0) for f in field]
        gc = [jnp.where(ok_c, pltpu.roll(f, w - 1, 1) - f, 0.0) for f in field]
        inv = lax.rsqrt(gr[0] * gr[0] + gc[0] * gc[0] + (gr[1] * gr[1] + gc[1] * gc[1]) + FLOOR_SQ)
        nxt = []
        for p in range(2):
            fr = gr[p] * inv
            fc = gc[p] * inv
            div = fr - pltpu.roll(fr, 1, 0) + fc - pltpu.roll(fc, 1, 1)
            nxt.append(field[p] - STEP * (field[p] - planes[p] - TV_WEIGHT * div))
        field = nxt
    for p in range(2):
        out_ref[p] = field[p][:TR, :512]


def refine(got, pos, norm, nrow, ncol):
    smem = pl.BlockSpec(memory_space=pltpu.SMEM)
    vmem = pl.BlockSpec(memory_space=pltpu.VMEM)
    return pl.pallas_call(
        functools.partial(refine_kernel, norm, nrow, ncol),
        out_shape=jax.ShapeDtypeStruct((2, TR, 512), F32),
        in_specs=[smem, vmem],
        out_specs=vmem,
        name="refine",
    )(pos, got)


def body(ny, nc, nx, nz, echoes, slope, shift, footprint, band_start, row_phase):
    x = lax.axis_index("x")
    z = lax.axis_index("z")
    y = lax.axis_index("y")
    core = lax.axis_index("c")
    tiles = nx * nz
    up = [(i, (i + 1) % nz) for i in range(nz)]
    down = [(i, (i - 1) % nz) for i in range(nz)]

    ech = echoes.reshape(2, 4, 128, 128).reshape(2, 512, 128)
    e0, e1 = ech[0], ech[1]
    pieces = {(0, 0): e0, (0, 1): e1}
    f = [e0, e1]
    b = [e0, e1]
    half = nz // 2
    for d in range(1, half + 1):
        for mem in range(2):
            if d < half or mem == 0:
                f[mem] = lax.ppermute(f[mem], "z", up)
                pieces[(d, mem)] = f[mem]
            if d < half or mem == 1:
                b[mem] = lax.ppermute(b[mem], "z", down)
                pieces[(nz - d, mem)] = b[mem]
    e_list = [pieces[(d, mem)] for d in range(nz) for mem in range(2)]

    par = jnp.concatenate([slope, shift], axis=1).astype(F32).reshape(8)
    par = jnp.pad(par, (0, TR - 8))
    small = jnp.stack([band_start.astype(F32), row_phase, par])
    small, _ = lax.optimization_barrier((small, pieces[(1, 0)]))
    for axis, me, size, dim in (("x", x, nx, 1), ("z", z, nz, 0)):
        bit = 1
        while bit < size:
            other = lax.ppermute(small, axis, [(i, i ^ bit) for i in range(size)])
            upper = (me & bit) != 0
            small = jnp.concatenate(
                [jnp.where(upper, other, small), jnp.where(upper, small, other)], axis=dim
            )
            bit *= 2
    t_re, t_im, a_re, a_im, bs = tables(jnp.stack([x, z]), small, nz)

    dist = jnp.arange(nz, dtype=jnp.int32)
    src = x * nz + jnp.mod(z - dist, nz)
    ids = (2 * src[:, None] + jnp.arange(2, dtype=jnp.int32)[None, :]).reshape(-1)
    own_tile = jnp.arange(nx, dtype=jnp.int32) * nz + z
    set_tile = jnp.concatenate([own_tile, own_tile - 1, own_tile + 1])
    which = set_tile[:, None] == jnp.arange(tiles, dtype=jnp.int32)[None, :]
    lists = jnp.sum(jnp.where(which[:, :, None], footprint[0][None] + 1, 0), axis=1) - 1
    used = jnp.any(lists[:, None, :] == ids[None, :, None], axis=2)
    order = jnp.arange(2 * nz, dtype=jnp.int32)
    before = order[None, :] < order[:, None]
    pos = jnp.sum((used[:, None, :] & before[None]).astype(jnp.int32), axis=2)
    cnt = jnp.minimum(jnp.sum(used.astype(jnp.int32), axis=1), nz)
    want = jnp.arange(nz, dtype=jnp.int32)
    lst = jnp.sum(
        jnp.where(used[:, None, :] & (pos[:, None, :] == want[None, :, None]), order[None, None, :], 0), axis=2
    )

    own, other = form_images(
        e_list, cubic_pair(), t_re, t_im, bs, cnt, lst.reshape(-1), core.reshape(1), a_re, a_im, nx
    )
    other = lax.ppermute(other, "c", [(0, 1), (1, 0)])
    mine = (own + other.astype(F32)).astype(BF16)
    got = lax.all_to_all(mine, ("x", "y"), 0, 0, tiled=True)
    groups = ny * nc
    norm = float(PB * tiles * groups) ** (-0.5)
    where_at = jnp.stack([(x * nz + z) * TR, (y * nc + core) * 512])
    return refine(got, where_at, norm, tiles * TR, NCOL)


def solution(mesh):
    nx, nz = 4, 8
    ny, nc = 4, 2
    fine = Mesh(mesh.devices.reshape(ny, nc, nx, nz), ("y", "c", "x", "z"))
    in_specs = (
        P(("y", "c", "x", "z"), None, None, None),
        P(("y", "c", "x", "z"), None),
        P(("y", "c", "x", "z"), None),
        P(("y", "c"), None, None),
        P(("x", "z")),
        P(("x", "z")),
    )
    out_specs = P(None, ("x", "z"), ("y", "c"))
    return jax.shard_map(
        functools.partial(body, ny, nc, nx, nz),
        mesh=fine,
        in_specs=in_specs,
        out_specs=out_specs,
        check_vma=False,
    )
```

```python
import functools

import jax
import jax.numpy as jnp
from jax import lax
from jax.experimental import pallas as pl
from jax.experimental.pallas import tpu as pltpu
from jax.sharding import Mesh, PartitionSpec as P

NCOL = 4096
PB = 2
ITERS = 2
TR = 32
STEP = 0.5
TV_WEIGHT = 0.4
FLOOR_SQ = 0.25
F32 = jnp.float32
BF16 = jnp.bfloat16
PITCH = 33
PIECE = 304
UNROLL = (8, 8, 8, 8, 8, 4, 4, 4)
DOT_ROWS = 4


def cubic_pair():
    j = lax.broadcasted_iota(jnp.int32, (256, 256), 0)
    c = lax.broadcasted_iota(jnp.int32, (256, 256), 1)
    same = (j < 128) == (c < 128)
    q = 3 * (c & 127) + 4
    f = (q & 3).astype(F32) / 4.0
    f2 = f * f
    f3 = f2 * f
    weights = [
        (-f3 + 2.0 * f2 - f) * 0.5,
        (3.0 * f3 - 5.0 * f2 + 2.0) * 0.5,
        (-3.0 * f3 + 4.0 * f2 + f) * 0.5,
        (f3 - f2) * 0.5,
    ]
    tap = (j & 127) - q // 4
    out = jnp.zeros((256, 256), F32)
    for shift, weight in zip(range(-1, 3), weights):
        out = out + jnp.where(same & (tap == shift), weight, 0.0)
    return out.astype(BF16)


def form_kernel(
    n_in, strips, slots, sets, bs_ref, cnt_ref, lst_ref, core_ref, are_ref, aim_ref, *refs
):
    e_refs = refs[:n_in]
    w_hbm, tre_hbm, tim_hbm, own_hbm, oth_hbm = refs[n_in : n_in + 5]
    e_b, w_ref, tre_ref, tim_ref, own_ref, oth_ref, e_s, o_s, in_sem, out_sem = refs[n_in + 5 :]
    arrive = [
        pltpu.make_async_copy(e, e_b.at[k], in_sem.at[k]) for k, e in enumerate(e_refs)
    ] + [
        pltpu.make_async_copy(src, dst, in_sem.at[n_in + k])
        for k, (src, dst) in enumerate(((w_hbm, w_ref), (tre_hbm, tre_ref), (tim_hbm, tim_ref)))
    ]
    for copy in arrive:
        copy.start()
    for k in range(n_in):
        arrive[k].wait()
        e_s[k * 512 : k * 512 + 512, :] = e_b[k].astype(F32)
    for copy in arrive[n_in:]:
        copy.wait()
    maxn = lst_ref.shape[0] // sets
    half_o = strips * 40 * PITCH
    lane = lax.broadcasted_iota(jnp.int32, (8, 128), 1)
    lane16 = lax.broadcasted_iota(jnp.int32, (16, 128), 1)

    def zero_rows(first, count):
        def step(k, carry):
            at = (first + k) * PITCH
            o_s[pl.ds(at, 32), :] = jnp.zeros((32, 128), F32)
            o_s[pl.ds(at + half_o, 32), :] = jnp.zeros((32, 128), F32)
            return carry

        lax.fori_loop(0, count, step, 0)

    for s in range(strips):
        zero_rows(s * 40 + 34, 4)

    def one_set(t, carry):
        cnt = cnt_ref[t]
        is_main = t < strips
        edge = t - strips
        strip = jnp.where(is_main, t, edge & (strips - 1))
        below = edge >= strips
        nrow = jnp.where(is_main, TR, 2)
        orow = strip * 40 + jnp.where(is_main, 0, jnp.where(below, 32, 38))
        part = jnp.where(is_main, 0, jnp.where(below, 2, 1))
        brow = strip * TR + jnp.where(part == 1, TR - 2, 0)
        acol = part * 128 + brow

        @pl.when(cnt == 0)
        def _():
            zero_rows(orow, nrow)

        for n, unroll in [(n, UNROLL[n - 1]) for n in range(1, maxn + 1)] + [
            (n, 2) for n in range(1, maxn + 1)
        ]:

            @pl.when((cnt == n) & (is_main if unroll > 2 else edge >= 0))
            def _(n=n, unroll=unroll):
                slot = [lst_ref[t * maxn + j] for j in range(n)]

                def some_rows(step, carry):
                    for u0 in range(0, unroll, DOT_ROWS):
                        left, right = [], []
                        for u in range(u0, min(u0 + DOT_ROWS, unroll)):
                            bs = bs_ref[part, brow + step * unroll + u]
                            for i in range(4):
                                start = bs + 96 * i
                                m = lax.shift_right_logical(start, 7)
                                o = start & 127
                                back = (128 - o) & 127
                                whole = lane16 < 128 - o
                                for j in range(n):
                                    for ri, side in ((0, left), (1, right)):
                                        at = slot[j] * 512 + ri * 128 + m
                                        lo, hi = [
                                            jnp.concatenate(
                                                [
                                                    e_s[pl.ds(at + t, 8, stride=3), :],
                                                    e_s[pl.ds(at + t + 256, 8, stride=3), :],
                                                ],
                                                axis=0,
                                            ).astype(BF16)
                                            for t in range(2)
                                        ]
                                        lo = pltpu.roll(lo, back, 1)
                                        hi = pltpu.roll(hi, back, 1)
                                        side.append(jnp.where(whole, lo, hi))
                        lhs = jnp.concatenate(
                            [jnp.concatenate(left, axis=0), jnp.concatenate(right, axis=0)], axis=1
                        )
                        res = jnp.dot(lhs, w_ref[...], preferred_element_type=F32)
                        for u in range(u0, min(u0 + DOT_ROWS, unroll)):
                            r = step * unroll + u
                            acc_re = [None] * 4
                            acc_im = [None] * 4
                            for j in range(n):
                                for p in range(2):
                                    pa = slot[j] * 2 + p
                                    a_re = are_ref[pa, acol + r]
                                    a_im = aim_ref[pa, acol + r]
                                    for i in range(4):
                                        t_re = tre_ref[pa, i]
                                        t_im = tim_ref[pa, i]
                                        b_re = a_re * t_re - a_im * t_im
                                        b_im = a_re * t_im + a_im * t_re
                                        row0 = ((((u - u0) * 4 + i) * n + j) * 2 + p) * 8
                                        x_re = res[row0 : row0 + 8, :128]
                                        x_im = res[row0 : row0 + 8, 128:]
                                        y_re = b_re * x_re - b_im * x_im
                                        y_im = b_re * x_im + b_im * x_re
                                        first = j == 0 and p == 0
                                        acc_re[i] = y_re if first else acc_re[i] + y_re
                                        acc_im[i] = y_im if first else acc_im[i] + y_im
                            for i in range(4):
                                at = (orow + r) * PITCH + i * 8
                                o_s[pl.ds(at, 8), :] = acc_re[i]
                                o_s[pl.ds(at + half_o, 8), :] = acc_im[i]
                    return carry

                lax.fori_loop(0, lax.shift_right_logical(nrow, unroll.bit_length() - 1), some_rows, 0)

        return carry

    lax.fori_loop(0, sets, one_set, 0)

    core = core_ref[0]
    sub = lax.broadcasted_iota(jnp.int32, (8, 128), 0)
    edge_rows = (sub < 2) | (sub >= 6)

    def pack(s, y, c):
        q = 2 * y + c
        base = s * (40 * PITCH) + q
        base_after = s * (40 * PITCH) + jnp.minimum(q + 1, 7)
        base_before = s * (40 * PITCH) + jnp.maximum(q - 1, 0)

        def fetch(plane, at, rg, i):
            return o_s[pl.ds(at + (plane * half_o + rg * 8 * PITCH + i * 8), 8, stride=PITCH), :]

        out = []
        for plane in range(2):
            for rg in range(4):
                for i in range(4):
                    out.append(fetch(plane, base, rg, i))
        for i in range(4):
            out.append(
                jnp.where(edge_rows, fetch(0, base, 4, i), pltpu.roll(fetch(1, base, 4, i), 4, 0))
            )
        cols = jnp.zeros((8, 128), F32)
        for plane in range(2):
            for rg in range(5):
                after = fetch(plane, base_after, rg, 0)
                before = fetch(plane, base_before, rg, 3)
                k = plane * 5 + rg
                both = pltpu.roll(jnp.where(lane < 64, after, before), 2 + 4 * k, 1)
                cols = jnp.where(lax.shift_right_logical(lane, 2) == k, both, cols)
        out.append(cols)
        out.append(jnp.zeros((8, 128), F32))
        return jnp.concatenate(out, axis=0)

    def pack_dest(d, carry):
        s = lax.shift_right_logical(d, 2)
        y = d & 3
        own_ref[d] = pack(s, y, core).astype(BF16)
        oth_ref[d] = pack(s, y, 1 - core).astype(BF16)
        for copy in leave(d):
            copy.start()
        return carry

    def leave(d):
        return (
            pltpu.make_async_copy(own_ref.at[d], own_hbm.at[d], out_sem.at[0, d]),
            pltpu.make_async_copy(oth_ref.at[d], oth_hbm.at[d], out_sem.at[1, d]),
        )

    def settle(d, carry):
        for copy in leave(d):
            copy.wait()
        return carry

    lax.fori_loop(0, strips * 4, pack_dest, 0)
    lax.fori_loop(0, strips * 4, settle, 0)


def form_images(e_list, w, t_re, t_im, bs, cnt, lst, core, a_re, a_im, strips):
    sets = cnt.shape[0]
    slots = t_re.shape[0] // 2
    smem = pl.BlockSpec(memory_space=pltpu.SMEM)
    n_in = len(e_list)
    dests = strips * 4
    return pl.pallas_call(
        functools.partial(form_kernel, n_in, strips, slots, sets),
        out_shape=(
            jax.ShapeDtypeStruct((dests, PIECE, 128), BF16),
            jax.ShapeDtypeStruct((dests, PIECE, 128), BF16),
        ),
        in_specs=[smem] * 6 + [pl.BlockSpec(memory_space=pl.ANY)] * (n_in + 3),
        out_specs=(pl.BlockSpec(memory_space=pl.ANY),) * 2,
        scratch_shapes=[
            pltpu.VMEM((n_in, 512, 128), BF16),
            pltpu.VMEM((256, 256), BF16),
            pltpu.VMEM(t_re.shape, F32),
            pltpu.VMEM(t_re.shape, F32),
            pltpu.VMEM((dests, PIECE, 128), BF16),
            pltpu.VMEM((dests, PIECE, 128), BF16),
            pltpu.VMEM((slots * 512, 128), F32),
            pltpu.VMEM((2 * strips * 40 * PITCH + 8, 128), F32),
            pltpu.SemaphoreType.DMA((n_in + 3,)),
            pltpu.SemaphoreType.DMA((2, dests)),
        ],
        compiler_params=pltpu.CompilerParams(vmem_limit_bytes=67043328),
        name="form_images",
    )(bs, cnt, lst, core, a_re, a_im, *e_list, w, t_re, t_im)


def tables_kernel(nz, at_ref, gs_ref, g_ref, tre_ref, tim_ref, are_ref, aim_ref, bs_ref):
    x, z = at_ref[0], at_ref[1]
    sub = lax.broadcasted_iota(jnp.int32, (8, 128), 0)
    lane = lax.broadcasted_iota(jnp.int32, (8, 128), 1)
    prev = lax.rem(z + nz - 1, nz)
    nxt = lax.rem(z + 1, nz)

    def lines(which):
        own = g_ref[pl.ds(3 * z + which, 1), :]
        above = g_ref[pl.ds(3 * prev + which, 1), :]
        below = g_ref[pl.ds(3 * nxt + which, 1), :]
        above = jnp.where(z == 0, pltpu.roll(above, 32, 1), above)
        below = jnp.where(z == nz - 1, pltpu.roll(below, 96, 1), below)
        return [jnp.broadcast_to(v, (8, 128)) for v in (own, above, below)]

    first = lines(0)
    bs_ref[...] = jnp.where(sub == 0, first[0], jnp.where(sub == 1, first[1], first[2])).astype(jnp.int32)
    phase = lines(1)
    place = (512 * sub + lane).astype(F32)
    for d in range(nz):
        src = 3 * lax.rem(z + nz - d, nz) + 2
        for mem in range(2):
            for p in range(2):
                k = (d * 2 + mem) * 2 + p
                slope = gs_ref[src, 32 * x + mem * 4 + p]
                ang = slope * place
                t_re, t_im = jnp.cos(ang), jnp.sin(ang)
                turn = jnp.full((8, 128), slope * 128.0, F32)
                e_re, e_im = jnp.cos(turn), jnp.sin(turn)
                for i in range(4):
                    tre_ref[k, i] = t_re
                    tim_ref[k, i] = t_im
                    if i < 3:
                        t_re, t_im = t_re * e_re - t_im * e_im, t_re * e_im + t_im * e_re
    for grp in range(nz // 2):
        shift = jnp.zeros((8, 128), F32)
        for row in range(8):
            k = grp * 8 + row
            d, mem, p = k // 4, (k // 2) % 2, k % 2
            src = 3 * lax.rem(z + nz - d, nz) + 2
            shift = jnp.where(sub == row, gs_ref[src, 32 * x + mem * 4 + 2 + p], shift)
        for part in range(3):
            ang = shift * phase[part]
            are_ref[grp * 8 : grp * 8 + 8, part * 128 : part * 128 + 128] = jnp.cos(ang)
            aim_ref[grp * 8 : grp * 8 + 8, part * 128 : part * 128 + 128] = jnp.sin(ang)


def tables(at, g, nz):
    smem = pl.BlockSpec(memory_space=pltpu.SMEM)
    vmem = pl.BlockSpec(memory_space=pltpu.VMEM)
    pulses = 4 * nz
    wave = jax.ShapeDtypeStruct((pulses, 4, 8, 128), F32)
    turn = jax.ShapeDtypeStruct((pulses, 384), F32)
    return pl.pallas_call(
        functools.partial(tables_kernel, nz),
        out_shape=(wave, wave, turn, turn, jax.ShapeDtypeStruct((8, 128), jnp.int32)),
        in_specs=[smem, smem, vmem],
        out_specs=(vmem,) * 5,
        name="tables",
    )(at, g, g)


def refine_kernel(norm, nrow, ncol, pos_ref, got_ref, out_ref):
    total = got_ref[0].astype(F32)
    for d in range(1, got_ref.shape[0]):
        total = total + got_ref[d].astype(F32)
    total = total * norm
    cols = total[288:296]
    planes = []
    for plane in range(2):
        rows = []
        for rg in range(5):
            if rg < 4:
                at = [((plane * 4 + rg) * 4 + i) * 8 for i in range(4)]
                line = [total[k : k + 8] for k in at]
            else:
                line = [total[256 + i * 8 : 264 + i * 8] for i in range(4)]
                if plane == 1:
                    line = [pltpu.roll(v, 4, 0) for v in line]
            k = plane * 5 + rg
            line.append(pltpu.roll(cols, (126 - 4 * k) % 128, 1))
            rows.append(jnp.concatenate(line, axis=1))
        planes.append(jnp.concatenate(rows, axis=0))
    h, w = 40, 640
    j = lax.broadcasted_iota(jnp.int32, (h, w), 0)
    c = lax.broadcasted_iota(jnp.int32, (h, w), 1)
    rid = pos_ref[0] + jnp.where(j >= 36, j - 40, j)
    cid = pos_ref[1] + jnp.where(c >= 576, c - 640, c)
    inside = (rid >= 0) & (cid >= 0) & (rid < nrow) & (cid < ncol)
    ok_r = inside & (rid < nrow - 1)
    ok_c = inside & (cid < ncol - 1)
    field = list(planes)
    for _ in range(ITERS):
        gr = [jnp.where(ok_r, pltpu.roll(f, h - 1, 0) - f, 0.0) for f in field]
        gc = [jnp.where(ok_c, pltpu.roll(f, w - 1, 1) - f, 0.0) for f in field]
        inv = lax.rsqrt(gr[0] * gr[0] + gc[0] * gc[0] + (gr[1] * gr[1] + gc[1] * gc[1]) + FLOOR_SQ)
        nxt = []
        for p in range(2):
            fr = gr[p] * inv
            fc = gc[p] * inv
            div = fr - pltpu.roll(fr, 1, 0) + fc - pltpu.roll(fc, 1, 1)
            nxt.append(field[p] - STEP * (field[p] - planes[p] - TV_WEIGHT * div))
        field = nxt
    for p in range(2):
        out_ref[p] = field[p][:TR, :512]


def refine(got, pos, norm, nrow, ncol):
    smem = pl.BlockSpec(memory_space=pltpu.SMEM)
    vmem = pl.BlockSpec(memory_space=pltpu.VMEM)
    return pl.pallas_call(
        functools.partial(refine_kernel, norm, nrow, ncol),
        out_shape=jax.ShapeDtypeStruct((2, TR, 512), F32),
        in_specs=[smem, vmem],
        out_specs=vmem,
        compiler_params=pltpu.CompilerParams(vmem_limit_bytes=16 * 1024 * 1024),
        name="refine",
    )(pos, got)


def body(ny, nc, nx, nz, echoes, slope, shift, footprint, band_start, row_phase):
    x = lax.axis_index("x")
    z = lax.axis_index("z")
    y = lax.axis_index("y")
    core = lax.axis_index("c")
    tiles = nx * nz
    up = [(i, (i + 1) % nz) for i in range(nz)]
    down = [(i, (i - 1) % nz) for i in range(nz)]

    ech = echoes.reshape(2, 4, 128, 128).reshape(2, 512, 128)
    par = jnp.concatenate([slope, shift], axis=1).astype(F32).reshape(8)
    par = jnp.pad(par, (0, TR - 8))
    small = jnp.stack([band_start.astype(F32), row_phase, par])
    doublings = [("x", x, nx, 1, 1), ("x", x, nx, 1, 2)] + [("z", z, nz, 0, 1 << k) for k in range(3)]

    def double(small, count):
        for axis, me, size, dim, bit in [doublings.pop(0) for _ in range(count)]:
            other = lax.ppermute(small, axis, [(i, i ^ bit) for i in range(size)])
            upper = (me & bit) != 0
            small = jnp.concatenate(
                [jnp.where(upper, other, small), jnp.where(upper, small, other)], axis=dim
            )
        return small

    e0, e1 = ech[0], ech[1]
    pieces = {(0, 0): e0, (0, 1): e1}
    f = [e0, e1]
    b = [e0, e1]
    half = nz // 2
    for d in range(1, half + 1):
        for mem in range(2):
            if d < half or mem == 0:
                f[mem] = lax.ppermute(f[mem], "z", up)
                pieces[(d, mem)] = f[mem]
            if d < half or mem == 1:
                b[mem] = lax.ppermute(b[mem], "z", down)
                pieces[(nz - d, mem)] = b[mem]
    small, _ = lax.optimization_barrier((small, pieces[(1, 0)]))
    waves = tables(jnp.stack([x, z]), double(small, 5), nz)
    t_re, t_im, a_re, a_im, bs = waves
    e_list = [pieces[(d, mem)] for d in range(nz) for mem in range(2)]

    dist = jnp.arange(nz, dtype=jnp.int32)
    src = x * nz + jnp.mod(z - dist, nz)
    ids = (2 * src[:, None] + jnp.arange(2, dtype=jnp.int32)[None, :]).reshape(-1)
    own_tile = jnp.arange(nx, dtype=jnp.int32) * nz + z
    set_tile = jnp.concatenate([own_tile, own_tile - 1, own_tile + 1])
    which = set_tile[:, None] == jnp.arange(tiles, dtype=jnp.int32)[None, :]
    lists = jnp.sum(jnp.where(which[:, :, None], footprint[0][None] + 1, 0), axis=1) - 1
    used = jnp.any(lists[:, None, :] == ids[None, :, None], axis=2)
    order = jnp.arange(2 * nz, dtype=jnp.int32)
    before = order[None, :] < order[:, None]
    pos = jnp.sum((used[:, None, :] & before[None]).astype(jnp.int32), axis=2)
    cnt = jnp.minimum(jnp.sum(used.astype(jnp.int32), axis=1), nz)
    want = jnp.arange(nz, dtype=jnp.int32)
    lst = jnp.sum(
        jnp.where(used[:, None, :] & (pos[:, None, :] == want[None, :, None]), order[None, None, :], 0), axis=2
    )

    own, other = form_images(
        e_list, cubic_pair(), t_re, t_im, bs, cnt, lst.reshape(-1), core.reshape(1), a_re, a_im, nx
    )
    other = lax.ppermute(other, "c", [(0, 1), (1, 0)])
    mine = (own.astype(F32) + other.astype(F32)).astype(BF16)
    got = lax.all_to_all(mine, ("x", "y"), 0, 0, tiled=True)
    groups = ny * nc
    norm = float(PB * tiles * groups) ** (-0.5)
    where_at = jnp.stack([(x * nz + z) * TR, (y * nc + core) * 512])
    return refine(got, where_at, norm, tiles * TR, NCOL)


def solution(mesh):
    nx, nz = 4, 8
    ny, nc = 4, 2
    fine = Mesh(mesh.devices.reshape(ny, nc, nx, nz), ("y", "c", "x", "z"))
    in_specs = (
        P(("y", "c", "x", "z"), None, None, None),
        P(("y", "c", "x", "z"), None),
        P(("y", "c", "x", "z"), None),
        P(("y", "c"), None, None),
        P(("x", "z")),
        P(("x", "z")),
    )
    out_specs = P(None, ("x", "z"), ("y", "c"))
    return jax.shard_map(
        functools.partial(body, ny, nc, nx, nz),
        mesh=fine,
        in_specs=in_specs,
        out_specs=out_specs,
        check_vma=False,
    )
```

```python
import functools

import jax
import jax.numpy as jnp
from jax import lax
from jax.experimental import pallas as pl
from jax.experimental.pallas import tpu as pltpu
from jax.sharding import Mesh, PartitionSpec as P

NCOL = 4096
PB = 2
ITERS = 2
TR = 32
STEP = 0.5
TV_WEIGHT = 0.4
FLOOR_SQ = 0.25
F32 = jnp.float32
BF16 = jnp.bfloat16
PITCH = 33
PIECE = 304
UNROLL = (8, 8, 8, 8, 8, 4, 4, 4)
DOT_ROWS = 4


def cubic_pair():
    j = lax.broadcasted_iota(jnp.int32, (256, 256), 0)
    c = lax.broadcasted_iota(jnp.int32, (256, 256), 1)
    same = (j < 128) == (c < 128)
    q = 3 * (c & 127) + 4
    f = (q & 3).astype(F32) / 4.0
    f2 = f * f
    f3 = f2 * f
    weights = [
        (-f3 + 2.0 * f2 - f) * 0.5,
        (3.0 * f3 - 5.0 * f2 + 2.0) * 0.5,
        (-3.0 * f3 + 4.0 * f2 + f) * 0.5,
        (f3 - f2) * 0.5,
    ]
    tap = (j & 127) - q // 4
    out = jnp.zeros((256, 256), F32)
    for shift, weight in zip(range(-1, 3), weights):
        out = out + jnp.where(same & (tap == shift), weight, 0.0)
    return out.astype(BF16)


def form_kernel(
    n_in, strips, slots, sets, bs_ref, cnt_ref, lst_ref, core_ref, are_ref, aim_ref, *refs
):
    e_refs = refs[:n_in]
    w_hbm, tre_hbm, tim_hbm, own_hbm, oth_hbm = refs[n_in : n_in + 5]
    e_b, w_ref, tre_ref, tim_ref, own_ref, oth_ref, e_s, o_s, in_sem, out_sem = refs[n_in + 5 :]
    arrive = [
        pltpu.make_async_copy(e, e_b.at[k], in_sem.at[k]) for k, e in enumerate(e_refs)
    ] + [
        pltpu.make_async_copy(src, dst, in_sem.at[n_in + k])
        for k, (src, dst) in enumerate(((w_hbm, w_ref), (tre_hbm, tre_ref), (tim_hbm, tim_ref)))
    ]
    for copy in arrive:
        copy.start()
    for k in range(n_in):
        arrive[k].wait()
        e_s[k * 512 : k * 512 + 512, :] = e_b[k].astype(F32)
    for copy in arrive[n_in:]:
        copy.wait()
    maxn = lst_ref.shape[0] // sets
    half_o = strips * 40 * PITCH
    lane = lax.broadcasted_iota(jnp.int32, (8, 128), 1)
    lane16 = lax.broadcasted_iota(jnp.int32, (16, 128), 1)

    def zero_rows(first, count):
        def step(k, carry):
            at = (first + k) * PITCH
            o_s[pl.ds(at, 32), :] = jnp.zeros((32, 128), F32)
            o_s[pl.ds(at + half_o, 32), :] = jnp.zeros((32, 128), F32)
            return carry

        lax.fori_loop(0, count, step, 0)

    for s in range(strips):
        zero_rows(s * 40 + 34, 4)

    def one_set(t, carry):
        cnt = cnt_ref[t]
        is_main = t < strips
        edge = t - strips
        strip = jnp.where(is_main, t, edge & (strips - 1))
        below = edge >= strips
        nrow = jnp.where(is_main, TR, 2)
        orow = strip * 40 + jnp.where(is_main, 0, jnp.where(below, 32, 38))
        part = jnp.where(is_main, 0, jnp.where(below, 2, 1))
        brow = strip * TR + jnp.where(part == 1, TR - 2, 0)
        acol = part * 128 + brow

        @pl.when(cnt == 0)
        def _():
            zero_rows(orow, nrow)

        for n, unroll in [(n, UNROLL[n - 1]) for n in range(1, maxn + 1)] + [
            (n, 2) for n in range(1, maxn + 1)
        ]:

            @pl.when((cnt == n) & (is_main if unroll > 2 else edge >= 0))
            def _(n=n, unroll=unroll):
                slot = [lst_ref[t * maxn + j] for j in range(n)]

                def some_rows(step, carry):
                    for u0 in range(0, unroll, DOT_ROWS):
                        left, right = [], []
                        for u in range(u0, min(u0 + DOT_ROWS, unroll)):
                            bs = bs_ref[part, brow + step * unroll + u]
                            for i in range(4):
                                start = bs + 96 * i
                                m = lax.shift_right_logical(start, 7)
                                o = start & 127
                                back = (128 - o) & 127
                                whole = lane16 < 128 - o
                                for j in range(n):
                                    for ri, side in ((0, left), (1, right)):
                                        at = slot[j] * 512 + ri * 128 + m
                                        lo, hi = [
                                            jnp.concatenate(
                                                [
                                                    e_s[pl.ds(at + t, 8, stride=3), :],
                                                    e_s[pl.ds(at + t + 256, 8, stride=3), :],
                                                ],
                                                axis=0,
                                            ).astype(BF16)
                                            for t in range(2)
                                        ]
                                        lo = pltpu.roll(lo, back, 1)
                                        hi = pltpu.roll(hi, back, 1)
                                        side.append(jnp.where(whole, lo, hi))
                        lhs = jnp.concatenate(
                            [jnp.concatenate(left, axis=0), jnp.concatenate(right, axis=0)], axis=1
                        )
                        res = jnp.dot(lhs, w_ref[...], preferred_element_type=F32)
                        for u in range(u0, min(u0 + DOT_ROWS, unroll)):
                            r = step * unroll + u
                            acc_re = [None] * 4
                            acc_im = [None] * 4
                            for j in range(n):
                                for p in range(2):
                                    pa = slot[j] * 2 + p
                                    a_re = are_ref[pa, acol + r]
                                    a_im = aim_ref[pa, acol + r]
                                    for i in range(4):
                                        t_re = tre_ref[pa, i]
                                        t_im = tim_ref[pa, i]
                                        b_re = a_re * t_re - a_im * t_im
                                        b_im = a_re * t_im + a_im * t_re
                                        row0 = ((((u - u0) * 4 + i) * n + j) * 2 + p) * 8
                                        x_re = res[row0 : row0 + 8, :128]
                                        x_im = res[row0 : row0 + 8, 128:]
                                        y_re = b_re * x_re - b_im * x_im
                                        y_im = b_re * x_im + b_im * x_re
                                        first = j == 0 and p == 0
                                        acc_re[i] = y_re if first else acc_re[i] + y_re
                                        acc_im[i] = y_im if first else acc_im[i] + y_im
                            for i in range(4):
                                at = (orow + r) * PITCH + i * 8
                                o_s[pl.ds(at, 8), :] = acc_re[i]
                                o_s[pl.ds(at + half_o, 8), :] = acc_im[i]
                    return carry

                lax.fori_loop(0, lax.shift_right_logical(nrow, unroll.bit_length() - 1), some_rows, 0)

        return carry

    lax.fori_loop(0, sets, one_set, 0)

    core = core_ref[0]
    sub = lax.broadcasted_iota(jnp.int32, (8, 128), 0)
    edge_rows = (sub < 2) | (sub >= 6)

    def pack(s, y, c):
        q = 2 * y + c
        base = s * (40 * PITCH) + q
        base_after = s * (40 * PITCH) + jnp.minimum(q + 1, 7)
        base_before = s * (40 * PITCH) + jnp.maximum(q - 1, 0)

        def fetch(plane, at, rg, i):
            return o_s[pl.ds(at + (plane * half_o + rg * 8 * PITCH + i * 8), 8, stride=PITCH), :]

        out = []
        for plane in range(2):
            for rg in range(4):
                for i in range(4):
                    out.append(fetch(plane, base, rg, i))
        for i in range(4):
            out.append(
                jnp.where(edge_rows, fetch(0, base, 4, i), pltpu.roll(fetch(1, base, 4, i), 4, 0))
            )
        cols = jnp.zeros((8, 128), F32)
        for plane in range(2):
            for rg in range(5):
                after = fetch(plane, base_after, rg, 0)
                before = fetch(plane, base_before, rg, 3)
                k = plane * 5 + rg
                both = pltpu.roll(jnp.where(lane < 64, after, before), 2 + 4 * k, 1)
                cols = jnp.where(lax.shift_right_logical(lane, 2) == k, both, cols)
        out.append(cols)
        out.append(jnp.zeros((8, 128), F32))
        return jnp.concatenate(out, axis=0)

    def pack_dest(d, carry):
        s = lax.shift_right_logical(d, 2)
        y = d & 3
        own_ref[d] = pack(s, y, core).astype(BF16)
        oth_ref[d] = pack(s, y, 1 - core).astype(BF16)
        for copy in leave(d):
            copy.start()
        return carry

    def leave(d):
        return (
            pltpu.make_async_copy(own_ref.at[d], own_hbm.at[d], out_sem.at[0, d]),
            pltpu.make_async_copy(oth_ref.at[d], oth_hbm.at[d], out_sem.at[1, d]),
        )

    def settle(d, carry):
        for copy in leave(d):
            copy.wait()
        return carry

    lax.fori_loop(0, strips * 4, pack_dest, 0)
    lax.fori_loop(0, strips * 4, settle, 0)


def form_images(e_list, w, t_re, t_im, bs, cnt, lst, core, a_re, a_im, strips):
    sets = cnt.shape[0]
    slots = t_re.shape[0] // 2
    smem = pl.BlockSpec(memory_space=pltpu.SMEM)
    n_in = len(e_list)
    dests = strips * 4
    return pl.pallas_call(
        functools.partial(form_kernel, n_in, strips, slots, sets),
        out_shape=(
            jax.ShapeDtypeStruct((dests, PIECE, 128), BF16),
            jax.ShapeDtypeStruct((dests, PIECE, 128), BF16),
        ),
        in_specs=[smem] * 6 + [pl.BlockSpec(memory_space=pl.ANY)] * (n_in + 3),
        out_specs=(pl.BlockSpec(memory_space=pl.ANY),) * 2,
        scratch_shapes=[
            pltpu.VMEM((n_in, 512, 128), BF16),
            pltpu.VMEM((256, 256), BF16),
            pltpu.VMEM(t_re.shape, F32),
            pltpu.VMEM(t_re.shape, F32),
            pltpu.VMEM((dests, PIECE, 128), BF16),
            pltpu.VMEM((dests, PIECE, 128), BF16),
            pltpu.VMEM((slots * 512, 128), F32),
            pltpu.VMEM((2 * strips * 40 * PITCH + 8, 128), F32),
            pltpu.SemaphoreType.DMA((n_in + 3,)),
            pltpu.SemaphoreType.DMA((2, dests)),
        ],
        compiler_params=pltpu.CompilerParams(vmem_limit_bytes=67043328),
        name="form_images",
    )(bs, cnt, lst, core, a_re, a_im, *e_list, w, t_re, t_im)


def tables_kernel(nz, at_ref, gs_ref, g_ref, tre_ref, tim_ref, are_ref, aim_ref, bs_ref):
    x, z = at_ref[0], at_ref[1]
    sub = lax.broadcasted_iota(jnp.int32, (8, 128), 0)
    lane = lax.broadcasted_iota(jnp.int32, (8, 128), 1)
    prev = lax.rem(z + nz - 1, nz)
    nxt = lax.rem(z + 1, nz)

    def lines(which):
        own = g_ref[pl.ds(3 * z + which, 1), :]
        above = g_ref[pl.ds(3 * prev + which, 1), :]
        below = g_ref[pl.ds(3 * nxt + which, 1), :]
        above = jnp.where(z == 0, pltpu.roll(above, 32, 1), above)
        below = jnp.where(z == nz - 1, pltpu.roll(below, 96, 1), below)
        return [jnp.broadcast_to(v, (8, 128)) for v in (own, above, below)]

    first = lines(0)
    bs_ref[...] = jnp.where(sub == 0, first[0], jnp.where(sub == 1, first[1], first[2])).astype(jnp.int32)
    phase = lines(1)
    place = (512 * sub + lane).astype(F32)
    for d in range(nz):
        src = 3 * lax.rem(z + nz - d, nz) + 2
        for mem in range(2):
            for p in range(2):
                k = (d * 2 + mem) * 2 + p
                slope = gs_ref[src, 32 * x + mem * 4 + p]
                ang = slope * place
                t_re, t_im = jnp.cos(ang), jnp.sin(ang)
                turn = jnp.full((8, 128), slope * 128.0, F32)
                e_re, e_im = jnp.cos(turn), jnp.sin(turn)
                for i in range(4):
                    tre_ref[k, i] = t_re
                    tim_ref[k, i] = t_im
                    if i < 3:
                        t_re, t_im = t_re * e_re - t_im * e_im, t_re * e_im + t_im * e_re
    for grp in range(nz // 2):
        shift = jnp.zeros((8, 128), F32)
        for row in range(8):
            k = grp * 8 + row
            d, mem, p = k // 4, (k // 2) % 2, k % 2
            src = 3 * lax.rem(z + nz - d, nz) + 2
            shift = jnp.where(sub == row, gs_ref[src, 32 * x + mem * 4 + 2 + p], shift)
        for part in range(3):
            ang = shift * phase[part]
            are_ref[grp * 8 : grp * 8 + 8, part * 128 : part * 128 + 128] = jnp.cos(ang)
            aim_ref[grp * 8 : grp * 8 + 8, part * 128 : part * 128 + 128] = jnp.sin(ang)


def tables(at, g, nz):
    smem = pl.BlockSpec(memory_space=pltpu.SMEM)
    vmem = pl.BlockSpec(memory_space=pltpu.VMEM)
    pulses = 4 * nz
    wave = jax.ShapeDtypeStruct((pulses, 4, 8, 128), F32)
    turn = jax.ShapeDtypeStruct((pulses, 384), F32)
    return pl.pallas_call(
        functools.partial(tables_kernel, nz),
        out_shape=(wave, wave, turn, turn, jax.ShapeDtypeStruct((8, 128), jnp.int32)),
        in_specs=[smem, smem, vmem],
        out_specs=(vmem,) * 5,
        name="tables",
    )(at, g, g)


def refine_kernel(norm, nrow, ncol, pos_ref, got_ref, out_ref):
    total = got_ref[0].astype(F32)
    for d in range(1, got_ref.shape[0]):
        total = total + got_ref[d].astype(F32)
    total = total * norm
    cols = total[288:296]
    planes = []
    for plane in range(2):
        rows = []
        for rg in range(5):
            if rg < 4:
                at = [((plane * 4 + rg) * 4 + i) * 8 for i in range(4)]
                line = [total[k : k + 8] for k in at]
            else:
                line = [total[256 + i * 8 : 264 + i * 8] for i in range(4)]
                if plane == 1:
                    line = [pltpu.roll(v, 4, 0) for v in line]
            k = plane * 5 + rg
            line.append(pltpu.roll(cols, (126 - 4 * k) % 128, 1))
            rows.append(jnp.concatenate(line, axis=1))
        planes.append(jnp.concatenate(rows, axis=0))
    h, w = 40, 640
    j = lax.broadcasted_iota(jnp.int32, (h, w), 0)
    c = lax.broadcasted_iota(jnp.int32, (h, w), 1)
    rid = pos_ref[0] + jnp.where(j >= 36, j - 40, j)
    cid = pos_ref[1] + jnp.where(c >= 576, c - 640, c)
    inside = (rid >= 0) & (cid >= 0) & (rid < nrow) & (cid < ncol)
    ok_r = inside & (rid < nrow - 1)
    ok_c = inside & (cid < ncol - 1)
    field = list(planes)
    for _ in range(ITERS):
        gr = [jnp.where(ok_r, pltpu.roll(f, h - 1, 0) - f, 0.0) for f in field]
        gc = [jnp.where(ok_c, pltpu.roll(f, w - 1, 1) - f, 0.0) for f in field]
        inv = lax.rsqrt(gr[0] * gr[0] + gc[0] * gc[0] + (gr[1] * gr[1] + gc[1] * gc[1]) + FLOOR_SQ)
        nxt = []
        for p in range(2):
            fr = gr[p] * inv
            fc = gc[p] * inv
            div = fr - pltpu.roll(fr, 1, 0) + fc - pltpu.roll(fc, 1, 1)
            nxt.append(field[p] - STEP * (field[p] - planes[p] - TV_WEIGHT * div))
        field = nxt
    for p in range(2):
        out_ref[p] = field[p][:TR, :512]


def refine(got, pos, norm, nrow, ncol):
    smem = pl.BlockSpec(memory_space=pltpu.SMEM)
    vmem = pl.BlockSpec(memory_space=pltpu.VMEM)
    return pl.pallas_call(
        functools.partial(refine_kernel, norm, nrow, ncol),
        out_shape=jax.ShapeDtypeStruct((2, TR, 512), F32),
        in_specs=[smem, vmem],
        out_specs=vmem,
        compiler_params=pltpu.CompilerParams(vmem_limit_bytes=16 * 1024 * 1024),
        name="refine",
    )(pos, got)


def body(ny, nc, nx, nz, echoes, slope, shift, footprint, band_start, row_phase):
    x = lax.axis_index("x")
    z = lax.axis_index("z")
    y = lax.axis_index("y")
    core = lax.axis_index("c")
    tiles = nx * nz
    up = [(i, (i + 1) % nz) for i in range(nz)]
    down = [(i, (i - 1) % nz) for i in range(nz)]

    ech = echoes.reshape(2, 4, 128, 128).reshape(2, 512, 128)
    par = jnp.concatenate([slope, shift], axis=1).astype(F32).reshape(8)
    par = jnp.pad(par, (0, TR - 8))
    small = jnp.stack([band_start.astype(F32), row_phase, par])
    doublings = [("x", x, nx, 1, 1), ("x", x, nx, 1, 2)] + [("z", z, nz, 0, 1 << k) for k in range(3)]

    def double(small, count):
        for axis, me, size, dim, bit in [doublings.pop(0) for _ in range(count)]:
            other = lax.ppermute(small, axis, [(i, i ^ bit) for i in range(size)])
            upper = (me & bit) != 0
            small = jnp.concatenate(
                [jnp.where(upper, other, small), jnp.where(upper, small, other)], axis=dim
            )
        return small

    e0, e1 = ech[0], ech[1]
    pieces = {(0, 0): e0, (0, 1): e1}
    f = [e0, e1]
    b = [e0, e1]
    half = nz // 2
    for d in range(1, half + 1):
        for mem in range(2):
            if d < half or mem == 0:
                f[mem] = lax.ppermute(f[mem], "z", up)
                pieces[(d, mem)] = f[mem]
            if d < half or mem == 1:
                b[mem] = lax.ppermute(b[mem], "z", down)
                pieces[(nz - d, mem)] = b[mem]
    waves = tables(jnp.stack([x, z]), double(small, 5), nz)
    t_re, t_im, a_re, a_im, bs = waves
    e_list = [pieces[(d, mem)] for d in range(nz) for mem in range(2)]

    dist = jnp.arange(nz, dtype=jnp.int32)
    src = x * nz + jnp.mod(z - dist, nz)
    ids = (2 * src[:, None] + jnp.arange(2, dtype=jnp.int32)[None, :]).reshape(-1)
    own_tile = jnp.arange(nx, dtype=jnp.int32) * nz + z
    set_tile = jnp.concatenate([own_tile, own_tile - 1, own_tile + 1])
    which = set_tile[:, None] == jnp.arange(tiles, dtype=jnp.int32)[None, :]
    lists = jnp.sum(jnp.where(which[:, :, None], footprint[0][None] + 1, 0), axis=1) - 1
    used = jnp.any(lists[:, None, :] == ids[None, :, None], axis=2)
    order = jnp.arange(2 * nz, dtype=jnp.int32)
    before = order[None, :] < order[:, None]
    pos = jnp.sum((used[:, None, :] & before[None]).astype(jnp.int32), axis=2)
    cnt = jnp.minimum(jnp.sum(used.astype(jnp.int32), axis=1), nz)
    want = jnp.arange(nz, dtype=jnp.int32)
    lst = jnp.sum(
        jnp.where(used[:, None, :] & (pos[:, None, :] == want[None, :, None]), order[None, None, :], 0), axis=2
    )

    own, other = form_images(
        e_list, cubic_pair(), t_re, t_im, bs, cnt, lst.reshape(-1), core.reshape(1), a_re, a_im, nx
    )
    other = lax.ppermute(other, "c", [(0, 1), (1, 0)])
    mine = (own.astype(F32) + other.astype(F32)).astype(BF16)
    got = lax.all_to_all(mine, ("x", "y"), 0, 0, tiled=True)
    groups = ny * nc
    norm = float(PB * tiles * groups) ** (-0.5)
    where_at = jnp.stack([(x * nz + z) * TR, (y * nc + core) * 512])
    return refine(got, where_at, norm, tiles * TR, NCOL)


def solution(mesh):
    nx, nz = 4, 8
    ny, nc = 4, 2
    fine = Mesh(mesh.devices.reshape(ny, nc, nx, nz), ("y", "c", "x", "z"))
    in_specs = (
        P(("y", "c", "x", "z"), None, None, None),
        P(("y", "c", "x", "z"), None),
        P(("y", "c", "x", "z"), None),
        P(("y", "c"), None, None),
        P(("x", "z")),
        P(("x", "z")),
    )
    out_specs = P(None, ("x", "z"), ("y", "c"))
    return jax.shard_map(
        functools.partial(body, ny, nc, nx, nz),
        mesh=fine,
        in_specs=in_specs,
        out_specs=out_specs,
        check_vma=False,
    )
```
